256 devices in a mesh: row: 16 (over x, z_lo, core), col: 16 (over y, z_hi).
Axes of the slice: x: 4, y: 4, z: 8 (z_hi: 4, z_lo: 2; z = z_hi * 2 + z_lo), core: 2. Of those that a mesh axis runs over, the one named last changes fastest.
Arguments:
- source: float32 [262144, 256], P(('row', 'col')), may hold values from -6 to 6
- leaf_in: float32 [1024, 128, 256], P(('row', 'col')), may hold values from -0.375 to 0.375
- factors: float32 [10, 1024, 128, 256], P(None, ('row', 'col')), may hold values from -0.375 to 0.375
- leaf_out: float32 [1024, 256, 128], P(('row', 'col')), may hold values from -0.5 to 0.5
- weight_table: float32 [1024, 256], P(('row', 'col')), may hold values from 0.25 to 4
- block_index: int32 [1024], P(('row', 'col')), may hold values from 0 to 1023
Outputs:
- result: float32 [262144, 256], P(('row', 'col'))
The draws below stay inside these ranges and needn't reach their ends.
All inputs are finite; a program needn't handle non-finite values.
Results may differ from the reference program's by a relative error of at most 0.0001.
Values sent between devices are 32-bit elements; how exact they have to be, the bound alone decides.
A program may use at most 64 MiB of HBM per device.

```python
import math
import jax
import jax.numpy as jnp
from jax import lax

LEAF = 256
RANK = 128
RHS = 256
LEVELS = 10
NODES = 1024


def set_ends(entries, stream_key, smallest, top_value):
    longest = entries.shape.index(max(entries.shape))
    spots = []
    for shift in (0, 1):
        where = [jax.random.randint(jax.random.fold_in(stream_key, axis), (), 0, length) for axis, length in enumerate(entries.shape)]
        where[longest] = (where[longest] + shift) % entries.shape[longest]
        spots.append(tuple(where))
    return entries.at[spots[0]].set(smallest).at[spots[1]].set(top_value)


def block_levels(own_key, dims, split, low, top_value):
    level, own = 1.0, jax.random.fold_in(own_key, 6)
    for axis_at, shards_of in split:
        heights = jnp.exp(jax.random.uniform(jax.random.fold_in(own, axis_at), (shards_of,), jnp.float32, low / len(split), top_value / len(split)))
        level = level * jnp.repeat(heights, dims[axis_at] // shards_of).reshape([-1 if axis == axis_at else 1 for axis in range(len(dims))])
    return level


def normal_values(key, extent, spread, reach, pieces=(), held_as=jnp.bfloat16):
    values = jax.random.normal(key, extent, jnp.float32) * spread
    if len(pieces) > 0:
        values = block_levels(key, extent, pieces, -0.22, 0.18) * values
    return jnp.clip(values, min=-reach, max=reach).astype(held_as)


def setup_inputs(seed: int = 0) -> dict:
    splits = jax.random.split(jax.random.key(seed), 7)
    return {
        "source": normal_values(splits[0], (NODES * LEAF, RHS), 1.0, 6.0, ((0, 256),), jnp.float32),
        "leaf_in": normal_values(splits[1], (NODES, RANK, LEAF), LEAF ** -0.5, 0.375, ((0, 256),), jnp.float32),
        "factors": normal_values(splits[2], (LEVELS, NODES, RANK, 2 * RANK), (2 * RANK) ** -0.5, 0.375, ((1, 256),), jnp.float32),
        "leaf_out": normal_values(splits[3], (NODES, LEAF, RANK), RANK ** -0.5, 0.5, ((0, 256),), jnp.float32),
        "weight_table": jnp.clip(jnp.exp(math.log(4.0) - 2.7725887 * jax.random.uniform(splits[4], (NODES, LEAF), jnp.float32) ** block_levels(splits[4], (NODES, LEAF), ((0, 256),), -0.2, 0.2)), 0.25, 4.0),
        "block_index": set_ends(jax.random.randint(splits[5], (NODES,), 0, NODES), jax.random.fold_in(splits[5], 1), 0, NODES - 1).astype(jnp.int32),
    }


HIGH = lax.Precision.HIGHEST


def swap_nodes(blocks, level_index):
    stride = 1 << level_index
    node_count = blocks.shape[0]
    shaped = blocks.reshape(node_count // (2 * stride), 2, stride, blocks.shape[1], blocks.shape[2])
    return shaped[:, ::-1].reshape(blocks.shape)


def reference(source, leaf_in, factors, leaf_out, weight_table, block_index):
    level_count = factors.shape[0]
    leaves = source.reshape(NODES, LEAF, RHS)
    coefficients = jnp.einsum("nrk,nks->nrs", leaf_in, leaves, precision=HIGH)
    for level_index in range(level_count):
        stacked = jnp.concatenate([coefficients, swap_nodes(coefficients, level_index)], axis=1)
        coefficients = jnp.einsum("nrk,nks->nrs", factors[level_index], stacked, precision=HIGH)
    image = jnp.einsum("nlr,nrs->nls", leaf_out, coefficients, precision=HIGH)
    profiles = weight_table[block_index.astype(jnp.int32)]
    scaled = profiles[:, :, None] * image
    adjoint = jnp.einsum("nlr,nls->nrs", leaf_out, scaled, precision=HIGH)
    for level_index in reversed(range(level_count)):
        own_part = factors[level_index][:, :, :RANK]
        cross_part = factors[level_index][:, :, RANK:]
        cross_term = jnp.einsum("nrk,nrs->nks", cross_part, adjoint, precision=HIGH)
        adjoint = jnp.einsum("nrk,nrs->nks", own_part, adjoint, precision=HIGH) + swap_nodes(cross_term, level_index)
    result = jnp.einsum("nrl,nrs->nls", leaf_in, adjoint, precision=HIGH)
    return result.reshape(NODES * LEAF, RHS)
```

```python
import functools

import jax
import jax.numpy as jnp
from jax import lax
from jax.experimental import pallas as pl
from jax.experimental.pallas import tpu as pltpu
from jax.sharding import PartitionSpec as P

MESH = pl.DeviceIdType.MESH
F32, BF16 = jnp.float32, jnp.bfloat16

HOP = {2: 5.2, 3: 6.4, 4: 3.0, 5: 3.0, 6: 1.5, 7: 3.0, 8: 3.0, 9: 3.0}
INTERVAL = 5.0
LEAD = 3


def plan(levels):
    order = list(range(2, levels)) + list(range(levels - 1, 1, -1))
    at = [0.0]
    for level in order:
        at.append(at[-1] + HOP[level])
    delay = [int(t // INTERVAL) for t in at]
    inside = sorted(range(len(at)), key=lambda s: (at[s] % INTERVAL, -s))
    return order, delay, inside


def halves(value):
    high = value.astype(BF16)
    low = (value - high.astype(F32)).astype(BF16)
    return high, low


def stacked(value):
    return jnp.concatenate(halves(value), axis=0)


def nt(a, b):
    return lax.dot_general(a, b, (((1,), (1,)), ((), ())), preferred_element_type=F32)


def nn(a, b):
    return lax.dot_general(a, b, (((1,), (0,)), ((), ())), preferred_element_type=F32)


def forward(state, factor):
    r = factor.shape[0] // 2
    c = state.shape[0]
    full = nt(stacked(state), factor)
    return (full[:c, :r] + full[:c, r:]) + (full[c:, :r] + full[c:, r:])


def backward(state, factor):
    c = state.shape[0]
    high, low = halves(state)
    left = jnp.concatenate(
        [jnp.concatenate([high, high], axis=1), jnp.concatenate([low, low], axis=1)], axis=0
    )
    full = nn(left, factor)
    return full[:c] + full[c:]


def flip(value, bit):
    step = 1 << bit
    return value + step - 2 * step * lax.rem(lax.div(value, step), 2)


def kernel(
    levels, col_bits, row_bits,
    index_ref, source_ref, leaf_in_ref, factors_ref, leaf_out_ref, table_ref, result_ref,
    src_v, lin_v, lout_v, fac_v, fb_v, linb_v, gram_v, tab_v, send_v, recv_v, own_v, loc_v, out_v,
    send_sem, recv_sem, tsend_sem, trecv_sem, fac_sem, src_sem, lin_sem, lout_sem, tab_sem, out_sem,
):
    nodes = 4
    chunks = 8
    rank = 128
    row, col = lax.axis_index("row"), lax.axis_index("col")
    device = row * (1 << col_bits) + col
    order, delay, inside = plan(levels)
    exchanges = len(order)
    half_way = exchanges // 2

    def partner(level):
        bit = level - 2
        if bit < col_bits:
            return (row, flip(col, bit))
        return (flip(row, bit - col_bits), col)

    def load_source(n):
        return pltpu.make_async_copy(source_ref.at[pl.ds(n * 256, 256)], src_v.at[n], src_sem.at[n])

    def load_leaf_in(n):
        return pltpu.make_async_copy(leaf_in_ref.at[n], lin_v.at[n], lin_sem.at[n])

    def load_factor(level, n):
        return pltpu.make_async_copy(factors_ref.at[level, n], fac_v.at[level, n], fac_sem.at[level, n])

    def load_leaf_out(n):
        return pltpu.make_async_copy(leaf_out_ref.at[n], lout_v.at[n], lout_sem.at[n])

    def load_table(n):
        return pltpu.make_async_copy(table_ref.at[pl.ds(n, 1)], tab_v.at[device * 4 + n], tab_sem.at[n])

    for n in range(nodes):
        load_table(n).start()
    for n in range(nodes):
        load_leaf_in(n).start()
        load_source(n).start()
    for level in range(levels):
        for n in range(nodes):
            load_factor(level, n).start()
    for n in range(nodes):
        load_leaf_out(n).start()

    barrier = pltpu.get_barrier_semaphore()
    for level in range(2, levels):
        pl.semaphore_signal(barrier, inc=1, device_id=partner(level), device_id_type=MESH)
    pl.semaphore_wait(barrier, levels - 2)

    def exchange(e, c):
        return pltpu.make_async_remote_copy(
            src_ref=send_v.at[e, c],
            dst_ref=recv_v.at[e, c],
            send_sem=send_sem.at[e, c],
            recv_sem=recv_sem.at[e, c],
            device_id=partner(order[e]),
            device_id_type=MESH,
        )

    def gather(k):
        size = 4 << k
        start = lax.div(device * 4, size) * size
        return pltpu.make_async_remote_copy(
            src_ref=tab_v.at[pl.ds(start, size)],
            dst_ref=tab_v.at[pl.ds(start, size)],
            send_sem=tsend_sem.at[k],
            recv_sem=trecv_sem.at[k],
            device_id=partner(k + 2),
            device_id_type=MESH,
        )

    def split_factor(level, n):
        load_factor(level, n).wait()
        fb_v[level, n] = stacked(fac_v[level, n])

    def start_leaf(h):
        for n in range(nodes):
            @pl.when(h == 0)
            def _():
                load_leaf_in(n).wait()
                load_source(n).wait()
                linb_v[n] = stacked(lin_v[n])
            x = src_v[n, :, pl.ds(pl.multiple_of(h * 128, 128), 128)]
            full = nn(linb_v[n], jnp.concatenate(halves(x), axis=1))
            coef = (full[:rank, :128] + full[:rank, 128:]) + (full[rank:, :128] + full[rank:, 128:])
            loc_v[0, n] = coef.T

    def start_level(level, h):
        for n in range(nodes):
            @pl.when(h == 0)
            def _():
                split_factor(level, n)
            other = n ^ (1 << level)
            new = forward(jnp.concatenate([loc_v[level, n], loc_v[level, other]], axis=1), fb_v[level, n])
            if level == 0:
                loc_v[1, n] = new
            else:
                send_v[0, h * 4 + n] = new

    def finish(n, h, state):
        both = backward(state, fb_v[1, n])
        loc_v[2, n] = both[:, :rank]
        loc_v[3, n] = both[:, rank:]

        for m in (0, 1):
            @pl.when(n == m + 2)
            def _():
                for q in (m, m + 2):
                    both = backward(loc_v[2, q] + loc_v[3, q ^ 2], fb_v[0, q])
                    loc_v[4, q] = both[:, :rank]
                    loc_v[5, q] = both[:, rank:]

        @pl.when(n == 3)
        def _():
            for q in range(nodes):
                block = backward(loc_v[4, q] + loc_v[5, q ^ 1], linb_v[q])
                out_v[h, q] = block.T
                store(h, q).start()

    def store(h, q):
        lanes = pl.ds(h * 128, 128) if isinstance(h, int) else pl.ds(pl.multiple_of(h * 128, 128), 128)
        return pltpu.make_async_copy(out_v.at[h, q], result_ref.at[pl.ds(q * 256, 256), lanes], out_sem.at[h, q])

    def make_gram(n):
        load_leaf_out(n).wait()
        leaf = lout_v[n]
        profile = tab_v[index_ref[n]]
        weighted = leaf.T * profile
        full = nn(stacked(weighted), jnp.concatenate(halves(leaf), axis=1))
        gram = (full[:rank, :rank] + full[:rank, rank:]) + (full[rank:, :rank] + full[rank:, rank:])
        gram_v[n] = stacked(gram)

    def step(s, c):
        n = lax.rem(c, 4)
        if s >= 1:
            exchange(s - 1, c).wait_recv()
        if s >= 2:
            exchange(s - 2, c).wait_send()
        if s == 0:
            exchange(0, c).start()
        elif s <= half_way:
            level = order[s - 1]

            @pl.when(c < 4)
            def _():
                split_factor(level, n)

            new = forward(jnp.concatenate([send_v[s - 1, c], recv_v[s - 1, c]], axis=1), fb_v[level, n])
            if s < half_way:
                send_v[s, c] = new
                exchange(s, c).start()
            else:
                @pl.when(c == 0)
                def _():
                    gather(levels - 3).wait_recv()

                @pl.when(c < 4)
                def _():
                    make_gram(n)

                both = backward(backward(new, gram_v[n]), fb_v[level, n])
                own_v[c] = both[:, :rank]
                send_v[s, c] = both[:, rank:]
                exchange(s, c).start()
        else:
            state = own_v[c] + recv_v[s - 1, c]
            if s < exchanges:
                level = order[s]
                both = backward(state, fb_v[level, n])
                own_v[c] = both[:, :rank]
                send_v[s, c] = both[:, rank:]
                exchange(s, c).start()
            else:
                finish(n, lax.div(c, 4), state)

    def iteration(i, carry):
        for first in (0, 4):
            @pl.when(i == first)
            def _():
                start_leaf(first // 4)

            @pl.when(i == first + 1)
            def _():
                start_level(0, first // 4)

            @pl.when(i == first + 2)
            def _():
                start_level(1, first // 4)
        for k in range(levels - 2):
            @pl.when(i == k)
            def _():
                if k == 0:
                    for n in range(nodes):
                        load_table(n).wait()
                else:
                    gather(k - 1).wait_recv()
                gather(k).start()
        for s in inside:
            c = i - (LEAD + delay[s])

            @pl.when(jnp.logical_and(c >= 0, c < chunks))
            def _():
                step(s, c)
        return carry

    lax.fori_loop(0, LEAD + chunks + max(delay), iteration, 0)

    def drain(c, carry):
        exchange(exchanges - 1, c).wait_send()
        return carry

    lax.fori_loop(0, chunks, drain, 0)
    for k in range(levels - 2):
        gather(k).wait_send()
    for h in range(2):
        for q in range(nodes):
            store(h, q).wait()


def body(source, leaf_in, factors, leaf_out, weight_table, block_index):
    levels = factors.shape[0]
    col_bits = lax.axis_size("col").bit_length() - 1
    row_bits = lax.axis_size("row").bit_length() - 1
    exchanges = 2 * (levels - 2)
    total = 4 << (levels - 2)
    anywhere = pl.BlockSpec(memory_space=pl.ANY)
    return pl.pallas_call(
        functools.partial(kernel, levels, col_bits, row_bits),
        out_shape=jax.ShapeDtypeStruct(source.shape, F32),
        in_specs=[pl.BlockSpec(memory_space=pltpu.SMEM)] + [anywhere] * 5,
        out_specs=anywhere,
        scratch_shapes=[
            pltpu.VMEM((4, 256, 256), F32),
            pltpu.VMEM((4, 128, 256), F32),
            pltpu.VMEM((4, 256, 128), F32),
            pltpu.VMEM((levels, 4, 128, 256), F32),
            pltpu.VMEM((levels, 4, 256, 256), BF16),
            pltpu.VMEM((4, 256, 256), BF16),
            pltpu.VMEM((4, 256, 128), BF16),
            pltpu.VMEM((total, 1, 256), F32),
            pltpu.VMEM((exchanges, 8, 128, 128), F32),
            pltpu.VMEM((exchanges, 8, 128, 128), F32),
            pltpu.VMEM((8, 128, 128), F32),
            pltpu.VMEM((6, 4, 128, 128), F32),
            pltpu.VMEM((2, 4, 256, 128), F32),
            pltpu.SemaphoreType.DMA((exchanges, 8)),
            pltpu.SemaphoreType.DMA((exchanges, 8)),
            pltpu.SemaphoreType.DMA((levels - 2,)),
            pltpu.SemaphoreType.DMA((levels - 2,)),
            pltpu.SemaphoreType.DMA((levels, 4)),
            pltpu.SemaphoreType.DMA((4,)),
            pltpu.SemaphoreType.DMA((4,)),
            pltpu.SemaphoreType.DMA((4,)),
            pltpu.SemaphoreType.DMA((4,)),
            pltpu.SemaphoreType.DMA((2, 4)),
        ],
        compiler_params=pltpu.CompilerParams(
            collective_id=0, has_side_effects=True, vmem_limit_bytes=60 << 20
        ),
        name="butterfly",
    )(block_index, source, leaf_in, factors, leaf_out, weight_table)


def solution(mesh):
    placed = (
        P(("row", "col"), None),
        P(("row", "col"), None, None),
        P(None, ("row", "col"), None, None),
        P(("row", "col"), None, None),
        P(("row", "col"), None),
        P(("row", "col")),
    )
    return jax.shard_map(
        body, mesh=mesh, in_specs=placed, out_specs=P(("row", "col"), None), check_vma=False
    )
```

```python
import functools

import jax
import jax.numpy as jnp
from jax import lax
from jax.experimental import pallas as pl
from jax.experimental.pallas import tpu as pltpu
from jax.sharding import PartitionSpec as P

MESH = pl.DeviceIdType.MESH
F32, BF16 = jnp.float32, jnp.bfloat16
NODES, RANK = 4, 128
WIDE = 64
CHUNKS = 256 // WIDE * NODES

HOP = {2: 5.0, 3: 6.2, 4: 3.0, 5: 3.6, 6: 1.8, 7: 3.2, 8: 3.0, 9: 3.8}
INTERVAL = 2.6
SECOND_AT = 9.0
GATHER = ((0, 1, 5), (2, 3), (6, 7), (4,))
GATHER_AT = (0.1, 10.0, 19.0, 31.0)
GRAM_AT = 38.0


def plan(levels):
    order = list(range(2, levels)) + list(range(levels - 1, 1, -1))
    at = [0.0]
    for level in order:
        at.append(at[-1] + HOP[level])
    steps = len(order) + 1
    events = [(c * INTERVAL + at[s], -s, s * CHUNKS + c) for s in range(steps) for c in range(CHUNKS)]
    events.append((SECOND_AT, 2, -1))
    base = steps * CHUNKS
    gram_at = min(GRAM_AT, at[len(order) // 2] - 0.01)
    rounds = len(gather_rounds(levels - 2))
    for k in range(rounds):
        events.append((min(GATHER_AT[k], gram_at - 0.1 + 0.01 * k), 1, base + k))
    for n in range(NODES):
        events.append((gram_at + n * INTERVAL, 1, base + rounds + n))
    return [code for _, _, code in sorted(events)]


def gather_rounds(bits):
    rounds, done = [], 0
    for group in GATHER:
        group = [b for b in group if b < bits]
        if group:
            masks = [sum(1 << b for i, b in enumerate(group) if m >> i & 1) for m in range(1, 1 << len(group))]
            rounds.append((done, masks))
            done += len(group)
    return rounds


def halves(value):
    high = value.astype(BF16)
    low = (value - high.astype(F32)).astype(BF16)
    return high, low


def stacked(value):
    return jnp.concatenate(halves(value), axis=0)


def nt(a, b):
    return lax.dot_general(a, b, (((1,), (1,)), ((), ())), preferred_element_type=F32)


def nn(a, b):
    return lax.dot_general(a, b, (((1,), (0,)), ((), ())), preferred_element_type=F32)


def quarters(full):
    m, k = full.shape[0] // 2, full.shape[1] // 2
    return (full[:m, :k] + full[:m, k:]) + (full[m:, :k] + full[m:, k:])


def forward(state, factor):
    return quarters(nt(stacked(state), factor))


def backward(state, factor):
    c = state.shape[0]
    high, low = halves(state)
    left = jnp.concatenate(
        [jnp.concatenate([high, high], axis=1), jnp.concatenate([low, low], axis=1)], axis=0
    )
    full = nn(left, factor)
    return full[:c] + full[c:]


def flip(value, bit):
    step = 1 << bit
    return value + step - 2 * step * lax.rem(lax.div(value, step), 2)


def kernel(
    levels, col_bits,
    index_ref, source_ref, leaf_in_ref, factors_ref, leaf_out_ref, table_ref, result_ref,
    src_v, lin_v, lout_v, fac_v, fb_v, linb_v, gram_v, tab_v, send_v, recv_v, own_v, loc_v, out_v,
    send_sem, recv_sem, tsend_sem, trecv_sem, fac_sem, src_sem, lin_sem, lout_sem, tab_sem, out_sem,
):
    bits = levels - 2
    cols = 1 << col_bits
    row, col = lax.axis_index("row"), lax.axis_index("col")
    device = row * cols + col
    exchanges = 2 * bits
    events = plan(levels)
    gather_bits = [b for group in GATHER for b in group if b < bits]
    rounds = gather_rounds(bits)

    def place(index):
        spot = 0
        for k, b in enumerate(gather_bits):
            spot = spot + lax.rem(lax.div(index, 1 << b), 2) * (1 << k)
        return spot

    def load_source(h, n):
        return pltpu.make_async_copy(
            source_ref.at[pl.ds(n * 256, 256), pl.ds(h * 128, 128)], src_v.at[h, n], src_sem.at[h, n]
        )

    def load_leaf_in(n):
        return pltpu.make_async_copy(leaf_in_ref.at[n], lin_v.at[n], lin_sem.at[n])

    def load_factor(level, n):
        return pltpu.make_async_copy(factors_ref.at[level, n], fac_v.at[level, n], fac_sem.at[level, n])

    def load_leaf_out(n):
        return pltpu.make_async_copy(leaf_out_ref.at[n], lout_v.at[n], lout_sem.at[n])

    mine = place(device)

    def load_table(n):
        return pltpu.make_async_copy(table_ref.at[pl.ds(n, 1)], tab_v.at[mine * NODES + n], tab_sem.at[n])

    def mate(mask):
        other = device
        for b in range(bits):
            if mask >> b & 1:
                other = flip(other, b)
        return (lax.div(other, cols), lax.rem(other, cols))

    barrier = pltpu.get_barrier_semaphore()
    mates = sorted({1 << b for b in range(bits)} | {mask for _, masks in rounds for mask in masks})
    for mask in mates:
        pl.semaphore_signal(barrier, inc=1, device_id=mate(mask), device_id_type=MESH)

    for n in range(NODES):
        load_leaf_in(n).start()
        load_source(0, n).start()
    for level in range(2):
        for n in range(NODES):
            load_factor(level, n).start()
    for n in range(NODES):
        load_table(n).start()

    def exchange(e, slot):
        b = e if e < bits else exchanges - 1 - e
        return pltpu.make_async_remote_copy(
            src_ref=send_v.at[slot],
            dst_ref=recv_v.at[slot],
            send_sem=send_sem.at[slot],
            recv_sem=recv_sem.at[slot],
            device_id=mate(1 << b),
            device_id_type=MESH,
        )

    def gather(k):
        done, masks = rounds[k]
        size = 1 << done
        rows = pl.ds(lax.div(mine, size) * size * NODES, size * NODES)
        return [
            pltpu.make_async_remote_copy(
                src_ref=tab_v.at[rows],
                dst_ref=tab_v.at[rows],
                send_sem=tsend_sem.at[mates.index(mask)],
                recv_sem=trecv_sem.at[mates.index(mask)],
                device_id=mate(mask),
                device_id_type=MESH,
            )
            for mask in masks
        ]

    def split_factor(level, n):
        load_factor(level, n).wait()
        fb_v[level, n] = stacked(fac_v[level, n])

    def store(h, q):
        lanes = pl.ds(h * 128, 128)
        return pltpu.make_async_copy(out_v.at[h, q], result_ref.at[pl.ds(q * 256, 256), lanes], out_sem.at[h, q])

    def start_half(h):
        for n in range(NODES):
            if h == 0:
                load_leaf_in(n).wait()
                linb_v[n] = stacked(lin_v[n])
            load_source(h, n).wait()
            loc_v[0, n] = quarters(nn(linb_v[n], jnp.concatenate(halves(src_v[h, n]), axis=1))).T
        for level in range(2):
            if h == 0:
                for n in range(NODES):
                    split_factor(level, n)
            for n in range(NODES):
                both = jnp.concatenate([loc_v[level, n], loc_v[level, n ^ (1 << level)]], axis=1)
                new = forward(both, fb_v[level, n])
                if level == 0:
                    loc_v[1, n] = new
                else:
                    for q in range(128 // WIDE):
                        send_v[(h * (128 // WIDE) + q) * NODES + n] = new[q * WIDE : (q + 1) * WIDE]

    def finish(c, state):
        n, q = c % NODES, c // NODES
        h, part = q * WIDE // 128, q % (128 // WIDE)
        rows = slice(part * WIDE, (part + 1) * WIDE)
        both = backward(state, fb_v[1, n])
        loc_v[2, n, rows] = both[:, :RANK]
        loc_v[3, n, rows] = both[:, RANK:]
        if n >= 2:
            for m in (n - 2, n):
                both = backward(loc_v[2, m, rows] + loc_v[3, m ^ 2, rows], fb_v[0, m])
                loc_v[4, m, rows] = both[:, :RANK]
                loc_v[5, m, rows] = both[:, RANK:]
        if n == 3 and rows.stop == 128:
            for m in range(NODES):
                block = backward(loc_v[4, m] + loc_v[5, m ^ 1], linb_v[m])
                out_v[h, m] = block.T
                store(h, m).start()

    def make_gram(n):
        load_leaf_out(n).wait()
        leaf = lout_v[n]
        index = index_ref[n]
        profile = tab_v[place(lax.div(index, NODES)) * NODES + lax.rem(index, NODES)]
        gram = quarters(nn(stacked(leaf.T * profile), jnp.concatenate(halves(leaf), axis=1)))
        gram_v[n] = stacked(gram)

    start_half(0)
    for n in range(NODES):
        load_factor(2, n).start()
        load_source(1, n).start()
    for level in range(3, levels):
        for n in range(NODES):
            load_factor(level, n).start()
    for n in range(NODES):
        load_leaf_out(n).start()
    for n in range(NODES):
        load_table(n).wait()
    pl.semaphore_wait(barrier, len(mates))

    def event(code):
        if code < 0:
            start_half(1)
            return
        s, c = code // CHUNKS, code % CHUNKS
        n, before = c % NODES, code - CHUNKS
        if s > exchanges:
            k = code - (exchanges + 1) * CHUNKS
            if 0 < k <= len(rounds):
                for copy in gather(k - 1):
                    copy.wait_recv()
            if k < len(rounds):
                for copy in gather(k):
                    copy.start()
            else:
                make_gram(k - len(rounds))
            return
        if s > 0:
            exchange(s - 1, before).wait_recv()
        if s < bits and s > 0:
            both = jnp.concatenate([send_v[before], recv_v[before]], axis=1)
            send_v[code] = forward(both, fb_v[s + 1, n])
        elif s == bits:
            both = jnp.concatenate([send_v[before], recv_v[before]], axis=1)
            new = forward(both, fb_v[levels - 1, n])
            both = backward(backward(new, gram_v[n]), fb_v[levels - 1, n])
            own_v[c] = both[:, :RANK]
            send_v[code] = both[:, RANK:]
        elif s > bits and s < exchanges:
            both = backward(own_v[c] + recv_v[before], fb_v[exchanges + 1 - s, n])
            own_v[c] = both[:, :RANK]
            send_v[code] = both[:, RANK:]
        if s < exchanges:
            exchange(s, code).start()
        else:
            finish(c, own_v[c] + recv_v[before])
        if s < bits and c < NODES:
            split_factor(s + 2, n)
        if s >= 2:
            exchange(s - 2, before - CHUNKS).wait_send()

    for code in events:
        event(code)

    def drain(c, carry):
        exchange(exchanges - 1, (exchanges - 1) * CHUNKS + c).wait_send()
        return carry

    lax.fori_loop(0, CHUNKS, drain, 0)
    for k in range(len(rounds)):
        for copy in gather(k):
            copy.wait_send()
    for h in range(2):
        for q in range(NODES):
            store(h, q).wait()


def body(source, leaf_in, factors, leaf_out, weight_table, block_index):
    levels = factors.shape[0]
    bits = levels - 2
    col_bits = lax.axis_size("col").bit_length() - 1
    slots = 2 * bits * CHUNKS
    mates = {1 << b for b in range(bits)} | {mask for _, masks in gather_rounds(bits) for mask in masks}
    anywhere = pl.BlockSpec(memory_space=pl.ANY)
    return pl.pallas_call(
        functools.partial(kernel, levels, col_bits),
        out_shape=jax.ShapeDtypeStruct(source.shape, F32),
        in_specs=[pl.BlockSpec(memory_space=pltpu.SMEM)] + [anywhere] * 5,
        out_specs=anywhere,
        scratch_shapes=[
            pltpu.VMEM((2, 4, 256, 128), F32),
            pltpu.VMEM((4, 128, 256), F32),
            pltpu.VMEM((4, 256, 128), F32),
            pltpu.VMEM((levels, 4, 128, 256), F32),
            pltpu.VMEM((levels, 4, 256, 256), BF16),
            pltpu.VMEM((4, 256, 256), BF16),
            pltpu.VMEM((4, 256, 128), BF16),
            pltpu.VMEM((NODES << bits, 1, 256), F32),
            pltpu.VMEM((slots, WIDE, RANK), F32),
            pltpu.VMEM((slots, WIDE, RANK), F32),
            pltpu.VMEM((CHUNKS, WIDE, RANK), F32),
            pltpu.VMEM((6, 4, 128, 128), F32),
            pltpu.VMEM((2, 4, 256, 128), F32),
            pltpu.SemaphoreType.DMA((slots,)),
            pltpu.SemaphoreType.DMA((slots,)),
            pltpu.SemaphoreType.DMA((len(mates),)),
            pltpu.SemaphoreType.DMA((len(mates),)),
            pltpu.SemaphoreType.DMA((levels, 4)),
            pltpu.SemaphoreType.DMA((2, 4)),
            pltpu.SemaphoreType.DMA((4,)),
            pltpu.SemaphoreType.DMA((4,)),
            pltpu.SemaphoreType.DMA((4,)),
            pltpu.SemaphoreType.DMA((2, 4)),
        ],
        compiler_params=pltpu.CompilerParams(
            collective_id=0, has_side_effects=True, vmem_limit_bytes=60 << 20
        ),
        name="butterfly",
    )(block_index, source, leaf_in, factors, leaf_out, weight_table)


def solution(mesh):
    placed = (
        P(("row", "col"), None),
        P(("row", "col"), None, None),
        P(None, ("row", "col"), None, None),
        P(("row", "col"), None, None),
        P(("row", "col"), None),
        P(("row", "col")),
    )
    return jax.shard_map(
        body, mesh=mesh, in_specs=placed, out_specs=P(("row", "col"), None), check_vma=False
    )
```

```python
import functools

import jax
import jax.numpy as jnp
from jax import lax
from jax.experimental import pallas as pl
from jax.experimental.pallas import tpu as pltpu
from jax.sharding import PartitionSpec as P

MESH = pl.DeviceIdType.MESH
F32, BF16 = jnp.float32, jnp.bfloat16
NODES, RANK = 4, 128
WIDE = 64
CHUNKS = 256 // WIDE * NODES

HOP = {2: 5.0, 3: 6.2, 4: 3.0, 5: 3.6, 6: 1.8, 7: 3.2, 8: 3.0, 9: 3.8}
INTERVAL = 2.6
SECOND_AT = 9.0
ORDER = (
    (0,), (1,), (2,), (272,), (16,), (3,), (17,), (4,), (273,), (18,), (5,), (32,), (19,), (6,),
    (-1,), (274,), (33,), (48,), (20,), (7,), (34,), (49,), (21,), (8,), (64,), (35,), (50,), (80,),
    (22,), (9,), (65,), (275,), (36,), (51,), (81,), (23, 96), (10,), (66,), (37,), (52,), (82,),
    (24, 97), (11,), (67,), (112,), (38,), (53,), (83,), (25, 98), (12,), (68,), (113,), (276,),
    (39,), (128, 54), (84,), (26, 99), (13,), (69,), (114,), (277,), (40,), (129, 55), (85,), (144,),
    (27, 100), (14,), (70,), (115,), (278,), (41,), (130, 56), (86,), (145,), (160,), (28, 101),
    (15,), (71,), (116,), (279,), (42,), (131, 57), (87,), (146,), (161,), (29, 102, 72), (176, 117),
    (43,), (132, 58), (88,), (147,), (162, 192), (30, 103, 73), (177, 118), (44,), (133, 59), (89,),
    (148,), (163, 193), (31, 104, 74), (178, 119), (208,), (45,), (134, 60), (90,), (149,),
    (164, 194), (105, 75), (179, 120), (209,), (46, 224), (135, 61), (91,), (150,), (165, 195),
    (106, 76), (180, 121), (210,), (47, 225), (136, 62), (92,), (151,), (166, 196), (107, 77),
    (181, 122), (211,), (226,), (137, 63), (93,), (152,), (167, 240, 197), (108, 78), (182, 123),
    (212,), (227,), (138,), (94,), (153,), (168, 241, 198), (109, 79), (183, 124), (213,), (228,),
    (139,), (95,), (154,), (169, 242, 199), (110,), (184, 125), (214,), (229,), (140,), (155,),
    (170, 243, 200), (111,), (185, 126), (215,), (230,), (141,), (156,), (171, 244, 201), (186, 127),
    (216,), (231,), (142,), (157,), (172, 245, 202), (187,), (217,), (232,), (143,), (158,),
    (173, 246, 203), (188,), (218,), (233,), (256,), (159,), (174, 247, 204), (189,), (219,), (234,),
    (257,), (175, 248, 205), (190,), (220,), (235,), (258,), (249, 206), (191,), (221,), (236,),
    (259,), (250, 207), (222,), (237,), (260,), (251,), (223,), (238,), (261,), (252,), (239,),
    (262,), (253,), (263,), (254,), (264,), (255,), (265,), (266,), (267,), (268,), (269,), (270,),
    (271,),
)
GATHER = ((0, 1, 5), (2, 3), (6, 7), (4,))
GATHER_AT = (0.1, 10.0, 19.0, 31.0)
GRAM_AT = 38.0


def plan(levels):
    if levels == 10:
        return ORDER
    order = list(range(2, levels)) + list(range(levels - 1, 1, -1))
    at = [0.0]
    for level in order:
        at.append(at[-1] + HOP[level])
    steps = len(order) + 1
    events = [(c * INTERVAL + at[s], -s, s * CHUNKS + c) for s in range(steps) for c in range(CHUNKS)]
    events.append((SECOND_AT, 2, -1))
    base = steps * CHUNKS
    gram_at = min(GRAM_AT, at[len(order) // 2] - 0.01)
    rounds = len(gather_rounds(levels - 2))
    for k in range(rounds):
        events.append((min(GATHER_AT[k], gram_at - 0.1 + 0.01 * k), 1, base + k))
    for n in range(NODES):
        events.append((gram_at + n * INTERVAL, 1, base + rounds + n))
    return [(code,) for _, _, code in sorted(events)]


def gather_rounds(bits):
    rounds, done = [], 0
    for group in GATHER:
        group = [b for b in group if b < bits]
        if group:
            masks = [sum(1 << b for i, b in enumerate(group) if m >> i & 1) for m in range(1, 1 << len(group))]
            rounds.append((done, masks))
            done += len(group)
    return rounds


def halves(value):
    high = value.astype(BF16)
    low = (value - high.astype(F32)).astype(BF16)
    return high, low


def stacked(value):
    return jnp.concatenate(halves(value), axis=0)


def nt(a, b):
    return lax.dot_general(a, b, (((1,), (1,)), ((), ())), preferred_element_type=F32)


def nn(a, b):
    return lax.dot_general(a, b, (((1,), (0,)), ((), ())), preferred_element_type=F32)


def quarters(full):
    m, k = full.shape[0] // 2, full.shape[1] // 2
    return (full[:m, :k] + full[:m, k:]) + (full[m:, :k] + full[m:, k:])


def forward(state, factor):
    return quarters(nt(stacked(state), factor))


def backward(state, factor):
    c = state.shape[0]
    high, low = halves(state)
    left = jnp.concatenate(
        [jnp.concatenate([high, high], axis=1), jnp.concatenate([low, low], axis=1)], axis=0
    )
    full = nn(left, factor)
    return full[:c] + full[c:]


def flip(value, bit):
    step = 1 << bit
    return value + step - 2 * step * lax.rem(lax.div(value, step), 2)


def kernel(
    levels, col_bits,
    index_ref, source_ref, leaf_in_ref, factors_ref, leaf_out_ref, table_ref, result_ref,
    src_v, lin_v, lout_v, fac_v, fb_v, linb_v, gram_v, tab_v, send_v, recv_v, own_v, loc_v,
    send_sem, recv_sem, tsend_sem, trecv_sem, fac_sem, src_sem, lin_sem, lout_sem, tab_sem,
):
    bits = levels - 2
    cols = 1 << col_bits
    row, col = lax.axis_index("row"), lax.axis_index("col")
    device = row * cols + col
    exchanges = 2 * bits
    gather_bits = [b for group in GATHER for b in group if b < bits]
    rounds = gather_rounds(bits)

    def place(index):
        spot = 0
        for k, b in enumerate(gather_bits):
            spot = spot + lax.rem(lax.div(index, 1 << b), 2) * (1 << k)
        return spot

    def load_source(h, n):
        return pltpu.make_async_copy(
            source_ref.at[pl.ds(n * 256, 256), pl.ds(h * 128, 128)], src_v.at[h, n], src_sem.at[h, n]
        )

    def load_leaf_in(n):
        return pltpu.make_async_copy(leaf_in_ref.at[n], lin_v.at[n], lin_sem.at[n])

    def load_factor(level, n):
        return pltpu.make_async_copy(factors_ref.at[level, n], fac_v.at[level, n], fac_sem.at[level, n])

    def load_leaf_out(n):
        return pltpu.make_async_copy(leaf_out_ref.at[n], lout_v.at[n], lout_sem.at[n])

    mine = place(device)

    def load_table(n):
        return pltpu.make_async_copy(table_ref.at[pl.ds(n, 1)], tab_v.at[mine * NODES + n], tab_sem.at[n])

    def mate(mask):
        other = device
        for b in range(bits):
            if mask >> b & 1:
                other = flip(other, b)
        return (lax.div(other, cols), lax.rem(other, cols))

    barrier = pltpu.get_barrier_semaphore()
    mates = sorted({1 << b for b in range(bits)} | {mask for _, masks in rounds for mask in masks})
    for mask in mates:
        pl.semaphore_signal(barrier, inc=1, device_id=mate(mask), device_id_type=MESH)

    for n in range(NODES):
        load_leaf_in(n).start()
        load_source(0, n).start()
    for level in range(2):
        for n in range(NODES):
            load_factor(level, n).start()
    for n in range(NODES):
        load_table(n).start()
        load_source(1, n).start()

    def exchange(e, slot):
        b = e if e < bits else exchanges - 1 - e
        return pltpu.make_async_remote_copy(
            src_ref=send_v.at[slot],
            dst_ref=recv_v.at[slot],
            send_sem=send_sem.at[slot],
            recv_sem=recv_sem.at[slot],
            device_id=mate(1 << b),
            device_id_type=MESH,
        )

    def gather(k):
        done, masks = rounds[k]
        size = 1 << done
        rows = pl.ds(lax.div(mine, size) * size * NODES, size * NODES)
        return [
            pltpu.make_async_remote_copy(
                src_ref=tab_v.at[rows],
                dst_ref=tab_v.at[rows],
                send_sem=tsend_sem.at[mates.index(mask)],
                recv_sem=trecv_sem.at[mates.index(mask)],
                device_id=mate(mask),
                device_id_type=MESH,
            )
            for mask in masks
        ]

    def split_factor(level, n):
        load_factor(level, n).wait()
        fb_v[level, n] = stacked(fac_v[level, n])

    def start_half(h):
        for n in range(NODES):
            if h == 0:
                load_leaf_in(n).wait()
                linb_v[n] = stacked(lin_v[n])
            load_source(h, n).wait()
            loc_v[0, n] = quarters(nn(linb_v[n], jnp.concatenate(halves(src_v[h, n]), axis=1))).T
        for level in range(2):
            if h == 0:
                for n in range(NODES):
                    split_factor(level, n)
            for n in range(NODES):
                both = jnp.concatenate([loc_v[level, n], loc_v[level, n ^ (1 << level)]], axis=1)
                new = forward(both, fb_v[level, n])
                if level == 0:
                    loc_v[1, n] = new
                else:
                    for q in range(128 // WIDE):
                        send_v[(h * (128 // WIDE) + q) * NODES + n] = new[q * WIDE : (q + 1) * WIDE]

    def finish(c, state):
        n, q = c % NODES, c // NODES
        h, part = q * WIDE // 128, q % (128 // WIDE)
        rows = slice(part * WIDE, (part + 1) * WIDE)
        both = backward(state, fb_v[1, n])
        loc_v[2, n, rows] = both[:, :RANK]
        loc_v[3, n, rows] = both[:, RANK:]
        if n >= 2:
            for m in (n - 2, n):
                both = backward(loc_v[2, m, rows] + loc_v[3, m ^ 2, rows], fb_v[0, m])
                loc_v[4, m, rows] = both[:, :RANK]
                loc_v[5, m, rows] = both[:, RANK:]
        if n == 3 and rows.stop == 128:
            for m in range(NODES):
                block = backward(loc_v[4, m] + loc_v[5, m ^ 1], linb_v[m])
                result_ref[m * 256 : (m + 1) * 256, h * 128 : (h + 1) * 128] = block.T

    def make_gram(n):
        load_leaf_out(n).wait()
        leaf = lout_v[n]
        index = index_ref[n]
        profile = tab_v[place(lax.div(index, NODES)) * NODES + lax.rem(index, NODES)]
        gram = quarters(nn(stacked(leaf.T * profile), jnp.concatenate(halves(leaf), axis=1)))
        gram_v[n] = stacked(gram)

    start_half(0)
    for level in range(2, levels):
        for n in range(NODES):
            load_factor(level, n).start()
    for n in range(NODES):
        load_leaf_out(n).start()
    for n in range(NODES):
        load_table(n).wait()
    pl.semaphore_wait(barrier, len(mates))

    def event(code):
        if code < 0:
            start_half(1)
            return
        s, c = code // CHUNKS, code % CHUNKS
        before = code - CHUNKS
        if s > exchanges:
            k = code - (exchanges + 1) * CHUNKS
            if 0 < k <= len(rounds):
                for copy in gather(k - 1):
                    copy.wait_recv()
            if k < len(rounds):
                for copy in gather(k):
                    copy.start()
            else:
                make_gram(k - len(rounds))
        elif s == 0:
            exchange(0, code).start()
            after(code)
        else:
            exchange(s - 1, before).wait_recv()
            finish(c, own_v[c] + recv_v[before])
            after(code)

    def compute(code):
        s, c = code // CHUNKS, code % CHUNKS
        n, before = c % NODES, code - CHUNKS
        if 0 < s <= bits:
            new = forward(jnp.concatenate([send_v[before], recv_v[before]], axis=1), fb_v[s + 1, n])
            if s < bits:
                return new
            return backward(backward(new, gram_v[n]), fb_v[levels - 1, n])
        return backward(own_v[c] + recv_v[before], fb_v[exchanges + 1 - s, n])

    def run(group):
        for code in group:
            exchange(code // CHUNKS - 1, code - CHUNKS).wait_recv()
        results = [compute(code) for code in group]
        for code, new in zip(group, results):
            s, c = code // CHUNKS, code % CHUNKS
            if s >= bits:
                own_v[c] = new[:, :RANK]
                new = new[:, RANK:]
            send_v[code] = new
            exchange(s, code).start()
        for code in group:
            after(code)

    def after(code):
        s, c = code // CHUNKS, code % CHUNKS
        if s < bits and c < NODES:
            split_factor(s + 2, c % NODES)
        if s >= 2:
            exchange(s - 2, code - 2 * CHUNKS).wait_send()

    for group in plan(levels):
        if len(group) > 1 or CHUNKS <= group[0] < exchanges * CHUNKS:
            run(group)
        else:
            event(group[0])

    def drain(c, carry):
        exchange(exchanges - 1, (exchanges - 1) * CHUNKS + c).wait_send()
        return carry

    lax.fori_loop(0, CHUNKS, drain, 0)
    for k in range(len(rounds)):
        for copy in gather(k):
            copy.wait_send()


def body(source, leaf_in, factors, leaf_out, weight_table, block_index):
    levels = factors.shape[0]
    bits = levels - 2
    col_bits = lax.axis_size("col").bit_length() - 1
    slots = 2 * bits * CHUNKS
    mates = {1 << b for b in range(bits)} | {mask for _, masks in gather_rounds(bits) for mask in masks}
    anywhere = pl.BlockSpec(memory_space=pl.ANY)
    return pl.pallas_call(
        functools.partial(kernel, levels, col_bits),
        out_shape=pltpu.VMEM(source.shape, F32),
        in_specs=[pl.BlockSpec(memory_space=pltpu.SMEM)] + [anywhere] * 5,
        out_specs=pl.BlockSpec(memory_space=pltpu.VMEM),
        scratch_shapes=[
            pltpu.VMEM((2, 4, 256, 128), F32),
            pltpu.VMEM((4, 128, 256), F32),
            pltpu.VMEM((4, 256, 128), F32),
            pltpu.VMEM((levels, 4, 128, 256), F32),
            pltpu.VMEM((levels, 4, 256, 256), BF16),
            pltpu.VMEM((4, 256, 256), BF16),
            pltpu.VMEM((4, 256, 128), BF16),
            pltpu.VMEM((NODES << bits, 1, 256), F32),
            pltpu.VMEM((slots, WIDE, RANK), F32),
            pltpu.VMEM((slots, WIDE, RANK), F32),
            pltpu.VMEM((CHUNKS, WIDE, RANK), F32),
            pltpu.VMEM((6, 4, 128, 128), F32),
            pltpu.SemaphoreType.DMA((slots,)),
            pltpu.SemaphoreType.DMA((slots,)),
            pltpu.SemaphoreType.DMA((len(mates),)),
            pltpu.SemaphoreType.DMA((len(mates),)),
            pltpu.SemaphoreType.DMA((levels, 4)),
            pltpu.SemaphoreType.DMA((2, 4)),
            pltpu.SemaphoreType.DMA((4,)),
            pltpu.SemaphoreType.DMA((4,)),
            pltpu.SemaphoreType.DMA((4,)),
        ],
        compiler_params=pltpu.CompilerParams(
            collective_id=0, has_side_effects=True, vmem_limit_bytes=60 << 20
        ),
        name="butterfly",
    )(block_index, source, leaf_in, factors, leaf_out, weight_table)


def solution(mesh):
    placed = (
        P(("row", "col"), None),
        P(("row", "col"), None, None),
        P(None, ("row", "col"), None, None),
        P(("row", "col"), None, None),
        P(("row", "col"), None),
        P(("row", "col")),
    )
    return jax.shard_map(
        body, mesh=mesh, in_specs=placed, out_specs=P(("row", "col"), None), check_vma=False
    )
```

```python
import functools

import jax
import jax.numpy as jnp
from jax import lax
from jax.experimental import pallas as pl
from jax.experimental.pallas import tpu as pltpu
from jax.sharding import PartitionSpec as P

MESH = pl.DeviceIdType.MESH
F32, BF16 = jnp.float32, jnp.bfloat16
NODES, RANK = 4, 128
WIDE = 64
CHUNKS = 256 // WIDE * NODES

HOP = {2: 5.0, 3: 6.2, 4: 3.0, 5: 3.6, 6: 1.8, 7: 3.2, 8: 3.0, 9: 3.8}
INTERVAL = 2.6
SECOND_AT = 9.0
ORDER = (
    (0,), (272,), (1,), (2,), (16,), (3,), (17,), (4,), (273,), (-1,), (18,), (5,), (32,), (19,),
    (6,), (33,), (48,), (274,), (20,), (7,), (34,), (49,), (21,), (8,), (64,), (35,), (50,), (80,),
    (22,), (9,), (65,), (36,), (51,), (81,), (23,), (66,), (10,), (96,), (37,), (275,), (52,), (82,),
    (24,), (67, 97), (11,), (112,), (38,), (53,), (83,), (25, 68), (98,), (12,), (113,), (276,),
    (39,), (128,), (54,), (84,), (69, 26, 99), (13,), (114,), (277,), (40,), (129,), (55,), (85,),
    (144,), (70, 100, 27), (14,), (115,), (278,), (41,), (130,), (56,), (86,), (145,), (71, 101),
    (160, 28), (15,), (116,), (279,), (42,), (131,), (57,), (87,), (146,), (72, 102), (161, 29),
    (117, 176), (43,), (132,), (58, 88), (192, 147), (73, 103, 162), (30,), (118, 177), (44,),
    (133,), (59, 89), (193, 148), (104, 74, 163), (31, 208), (119, 178), (45,), (134,), (60, 90),
    (194, 149), (164, 105, 75), (209, 224), (120, 179), (46,), (135,), (61, 91), (195, 150),
    (165, 106), (76,), (210, 225), (121, 180), (47,), (136,), (62, 92), (196, 151), (166,),
    (107, 77), (211, 226), (181, 122), (240,), (137,), (63, 93), (197, 152), (167,), (108, 78, 212),
    (227,), (182,), (123,), (241,), (138,), (94,), (198,), (153,), (168,), (109, 213, 79), (228,),
    (183,), (124,), (242,), (139,), (95,), (199,), (154,), (169,), (214, 110, 229), (184,), (125,),
    (243,), (140,), (200,), (155,), (170,), (215, 230), (111,), (185,), (126,), (244,), (141,),
    (201,), (156,), (171, 216), (231,), (186,), (127,), (245,), (142,), (202,), (157,), (172, 217),
    (232,), (187,), (246,), (143,), (203,), (158,), (173, 218), (233,), (188,), (247,), (204,),
    (159,), (174, 219), (234,), (189,), (248,), (205,), (175,), (256,), (220, 235), (190,), (249,),
    (206,), (257,), (221, 236), (191,), (250,), (207,), (258,), (222, 237), (251,), (259,),
    (223, 238), (252,), (260,), (239,), (253,), (261,), (254,), (262,), (255,), (263,), (264,),
    (265,), (266,), (267,), (268,), (269,), (270,), (271,),
)
GATHER = ((0, 1, 5), (2, 3), (6, 7), (4,))
GATHER_AT = (0.1, 10.0, 19.0, 31.0)
GRAM_AT = 38.0


def plan(levels):
    if levels == 10:
        return ORDER
    order = list(range(2, levels)) + list(range(levels - 1, 1, -1))
    at = [0.0]
    for level in order:
        at.append(at[-1] + HOP[level])
    steps = len(order) + 1
    events = [(c * INTERVAL + at[s], -s, s * CHUNKS + c) for s in range(steps) for c in range(CHUNKS)]
    events.append((SECOND_AT, 2, -1))
    base = steps * CHUNKS
    gram_at = min(GRAM_AT, at[len(order) // 2] - 0.01)
    rounds = len(gather_rounds(levels - 2))
    for k in range(rounds):
        events.append((min(GATHER_AT[k], gram_at - 0.1 + 0.01 * k), 1, base + k))
    for n in range(NODES):
        events.append((gram_at + n * INTERVAL, 1, base + rounds + n))
    return [(code,) for _, _, code in sorted(events)]


def gather_rounds(bits):
    rounds, done = [], 0
    for group in GATHER:
        group = [b for b in group if b < bits]
        if group:
            masks = [sum(1 << b for i, b in enumerate(group) if m >> i & 1) for m in range(1, 1 << len(group))]
            rounds.append((done, masks))
            done += len(group)
    return rounds


def halves(value):
    high = value.astype(BF16)
    low = (value - high.astype(F32)).astype(BF16)
    return high, low


def stacked(value):
    return jnp.concatenate(halves(value), axis=0)


def nt(a, b):
    return lax.dot_general(a, b, (((1,), (1,)), ((), ())), preferred_element_type=F32)


def nn(a, b):
    return lax.dot_general(a, b, (((1,), (0,)), ((), ())), preferred_element_type=F32)


def quarters(full):
    m, k = full.shape[0] // 2, full.shape[1] // 2
    return (full[:m, :k] + full[:m, k:]) + (full[m:, :k] + full[m:, k:])


def forward(state, factor):
    return quarters(nt(stacked(state), factor))


def backward(state, factor):
    c = state.shape[0]
    high, low = halves(state)
    left = jnp.concatenate(
        [jnp.concatenate([high, high], axis=1), jnp.concatenate([low, low], axis=1)], axis=0
    )
    full = nn(left, factor)
    return full[:c] + full[c:]


def flip(value, bit):
    step = 1 << bit
    return value + step - 2 * step * lax.rem(lax.div(value, step), 2)


def kernel(
    levels, col_bits,
    index_ref, source_ref, leaf_in_ref, factors_ref, leaf_out_ref, table_ref, result_ref,
    src_v, lin_v, lout_v, fac_v, fb_v, linb_v, gram_v, tab_v, send_v, recv_v, own_v, loc_v,
    send_sem, recv_sem, tsend_sem, trecv_sem, fac_sem, src_sem, lin_sem, lout_sem, tab_sem,
):
    bits = levels - 2
    cols = 1 << col_bits
    row, col = lax.axis_index("row"), lax.axis_index("col")
    device = row * cols + col
    exchanges = 2 * bits
    gather_bits = [b for group in GATHER for b in group if b < bits]
    rounds = gather_rounds(bits)

    def place(index):
        spot = 0
        for k, b in enumerate(gather_bits):
            spot = spot + lax.rem(lax.div(index, 1 << b), 2) * (1 << k)
        return spot

    def load_source(h, n):
        return pltpu.make_async_copy(
            source_ref.at[pl.ds(n * 256, 256), pl.ds(h * 128, 128)], src_v.at[h, n], src_sem.at[h, n]
        )

    def load_leaf_in(n):
        return pltpu.make_async_copy(leaf_in_ref.at[n], lin_v.at[n], lin_sem.at[n])

    def load_factor(level, n):
        return pltpu.make_async_copy(factors_ref.at[level, n], fac_v.at[level, n], fac_sem.at[level, n])

    def load_leaf_out(n):
        return pltpu.make_async_copy(leaf_out_ref.at[n], lout_v.at[n], lout_sem.at[n])

    mine = place(device)

    def load_table(n):
        return pltpu.make_async_copy(table_ref.at[pl.ds(n, 1)], tab_v.at[mine * NODES + n], tab_sem.at[n])

    def mate(mask):
        other = device
        for b in range(bits):
            if mask >> b & 1:
                other = flip(other, b)
        return (lax.div(other, cols), lax.rem(other, cols))

    barrier = pltpu.get_barrier_semaphore()
    mates = sorted({1 << b for b in range(bits)} | {mask for _, masks in rounds for mask in masks})
    for mask in mates:
        pl.semaphore_signal(barrier, inc=1, device_id=mate(mask), device_id_type=MESH)

    for n in range(NODES):
        load_leaf_in(n).start()
        load_source(0, n).start()
    for level in range(2):
        for n in range(NODES):
            load_factor(level, n).start()
    for n in range(NODES):
        load_table(n).start()
        load_source(1, n).start()

    def exchange(e, slot):
        b = e if e < bits else exchanges - 1 - e
        return pltpu.make_async_remote_copy(
            src_ref=send_v.at[slot],
            dst_ref=recv_v.at[slot],
            send_sem=send_sem.at[slot],
            recv_sem=recv_sem.at[slot],
            device_id=mate(1 << b),
            device_id_type=MESH,
        )

    def gather(k):
        done, masks = rounds[k]
        size = 1 << done
        rows = pl.ds(lax.div(mine, size) * size * NODES, size * NODES)
        return [
            pltpu.make_async_remote_copy(
                src_ref=tab_v.at[rows],
                dst_ref=tab_v.at[rows],
                send_sem=tsend_sem.at[mates.index(mask)],
                recv_sem=trecv_sem.at[mates.index(mask)],
                device_id=mate(mask),
                device_id_type=MESH,
            )
            for mask in masks
        ]

    def split_factor(level, n):
        load_factor(level, n).wait()
        fb_v[level, n] = stacked(fac_v[level, n])

    def start_half(h):
        for n in range(NODES):
            if h == 0:
                load_leaf_in(n).wait()
                linb_v[n] = stacked(lin_v[n])
            load_source(h, n).wait()
            loc_v[0, n] = quarters(nn(linb_v[n], jnp.concatenate(halves(src_v[h, n]), axis=1))).T
        for level in range(2):
            if h == 0:
                for n in range(NODES):
                    split_factor(level, n)
            for n in range(NODES):
                both = jnp.concatenate([loc_v[level, n], loc_v[level, n ^ (1 << level)]], axis=1)
                new = forward(both, fb_v[level, n])
                if level == 0:
                    loc_v[1, n] = new
                else:
                    for q in range(128 // WIDE):
                        send_v[(h * (128 // WIDE) + q) * NODES + n] = new[q * WIDE : (q + 1) * WIDE]

    def finish(c, state):
        n, q = c % NODES, c // NODES
        h, part = q * WIDE // 128, q % (128 // WIDE)
        rows = slice(part * WIDE, (part + 1) * WIDE)
        both = backward(state, fb_v[1, n])
        loc_v[2, n, rows] = both[:, :RANK]
        loc_v[3, n, rows] = both[:, RANK:]
        if n >= 2:
            for m in (n - 2, n):
                both = backward(loc_v[2, m, rows] + loc_v[3, m ^ 2, rows], fb_v[0, m])
                loc_v[4, m, rows] = both[:, :RANK]
                loc_v[5, m, rows] = both[:, RANK:]
        if n == 3 and rows.stop == 128:
            for m in range(NODES):
                block = backward(loc_v[4, m] + loc_v[5, m ^ 1], linb_v[m])
                result_ref[m * 256 : (m + 1) * 256, h * 128 : (h + 1) * 128] = block.T

    def make_gram(n):
        load_leaf_out(n).wait()
        leaf = lout_v[n]
        index = index_ref[n]
        profile = tab_v[place(lax.div(index, NODES)) * NODES + lax.rem(index, NODES)]
        gram = quarters(nn(stacked(leaf.T * profile), jnp.concatenate(halves(leaf), axis=1)))
        gram_v[n] = stacked(gram)

    start_half(0)
    for level in range(2, levels):
        for n in range(NODES):
            load_factor(level, n).start()
    for n in range(NODES):
        load_leaf_out(n).start()
    for n in range(NODES):
        load_table(n).wait()
    pl.semaphore_wait(barrier, len(mates))

    def event(code):
        if code < 0:
            start_half(1)
            return
        s, c = code // CHUNKS, code % CHUNKS
        before = code - CHUNKS
        if s > exchanges:
            k = code - (exchanges + 1) * CHUNKS
            if 0 < k <= len(rounds):
                for copy in gather(k - 1):
                    copy.wait_recv()
            if k < len(rounds):
                for copy in gather(k):
                    copy.start()
            else:
                make_gram(k - len(rounds))
        elif s == 0:
            exchange(0, code).start()
            after(code)
        else:
            exchange(s - 1, before).wait_recv()
            finish(c, own_v[c] + recv_v[before])
            after(code)

    def compute(code):
        s, c = code // CHUNKS, code % CHUNKS
        n, before = c % NODES, code - CHUNKS
        if 0 < s <= bits:
            new = forward(jnp.concatenate([send_v[before], recv_v[before]], axis=1), fb_v[s + 1, n])
            if s < bits:
                return new
            return backward(backward(new, gram_v[n]), fb_v[levels - 1, n])
        return backward(own_v[c] + recv_v[before], fb_v[exchanges + 1 - s, n])

    def run(group):
        for code in group:
            exchange(code // CHUNKS - 1, code - CHUNKS).wait_recv()
        results = [compute(code) for code in group]
        for code, new in zip(group, results):
            s, c = code // CHUNKS, code % CHUNKS
            if s >= bits:
                own_v[c] = new[:, :RANK]
                new = new[:, RANK:]
            send_v[code] = new
            exchange(s, code).start()
        for code in group:
            after(code)

    def after(code):
        s, c = code // CHUNKS, code % CHUNKS
        if s < bits and c < NODES:
            split_factor(s + 2, c % NODES)
        if s >= 2:
            exchange(s - 2, code - 2 * CHUNKS).wait_send()

    for group in plan(levels):
        if len(group) > 1 or CHUNKS <= group[0] < exchanges * CHUNKS:
            run(group)
        else:
            event(group[0])

    def drain(c, carry):
        exchange(exchanges - 1, (exchanges - 1) * CHUNKS + c).wait_send()
        return carry

    lax.fori_loop(0, CHUNKS, drain, 0)
    for k in range(len(rounds)):
        for copy in gather(k):
            copy.wait_send()


def body(source, leaf_in, factors, leaf_out, weight_table, block_index):
    levels = factors.shape[0]
    bits = levels - 2
    col_bits = lax.axis_size("col").bit_length() - 1
    slots = 2 * bits * CHUNKS
    mates = {1 << b for b in range(bits)} | {mask for _, masks in gather_rounds(bits) for mask in masks}
    anywhere = pl.BlockSpec(memory_space=pl.ANY)
    return pl.pallas_call(
        functools.partial(kernel, levels, col_bits),
        out_shape=pltpu.VMEM(source.shape, F32),
        in_specs=[pl.BlockSpec(memory_space=pltpu.SMEM)] + [anywhere] * 5,
        out_specs=pl.BlockSpec(memory_space=pltpu.VMEM),
        scratch_shapes=[
            pltpu.VMEM((2, 4, 256, 128), F32),
            pltpu.VMEM((4, 128, 256), F32),
            pltpu.VMEM((4, 256, 128), F32),
            pltpu.VMEM((levels, 4, 128, 256), F32),
            pltpu.VMEM((levels, 4, 256, 256), BF16),
            pltpu.VMEM((4, 256, 256), BF16),
            pltpu.VMEM((4, 256, 128), BF16),
            pltpu.VMEM((NODES << bits, 1, 256), F32),
            pltpu.VMEM((slots, WIDE, RANK), F32),
            pltpu.VMEM((slots, WIDE, RANK), F32),
            pltpu.VMEM((CHUNKS, WIDE, RANK), F32),
            pltpu.VMEM((6, 4, 128, 128), F32),
            pltpu.SemaphoreType.DMA((slots,)),
            pltpu.SemaphoreType.DMA((slots,)),
            pltpu.SemaphoreType.DMA((len(mates),)),
            pltpu.SemaphoreType.DMA((len(mates),)),
            pltpu.SemaphoreType.DMA((levels, 4)),
            pltpu.SemaphoreType.DMA((2, 4)),
            pltpu.SemaphoreType.DMA((4,)),
            pltpu.SemaphoreType.DMA((4,)),
            pltpu.SemaphoreType.DMA((4,)),
        ],
        compiler_params=pltpu.CompilerParams(
            collective_id=0, has_side_effects=True, vmem_limit_bytes=60 << 20
        ),
        name="butterfly",
    )(block_index, source, leaf_in, factors, leaf_out, weight_table)


def solution(mesh):
    placed = (
        P(("row", "col"), None),
        P(("row", "col"), None, None),
        P(None, ("row", "col"), None, None),
        P(("row", "col"), None, None),
        P(("row", "col"), None),
        P(("row", "col")),
    )
    return jax.shard_map(
        body, mesh=mesh, in_specs=placed, out_specs=P(("row", "col"), None), check_vma=False
    )
```
